512 devices in a mesh: energy: 32 (over z_hi, y, core), cell: 16 (over x, z_lo).
Axes of the slice: x: 4, y: 4, z: 16 (z_hi: 4, z_lo: 4; z = z_hi * 4 + z_lo), core: 2. Of those that a mesh axis runs over, the one named last changes fastest.
Arguments:
- g_retarded: bfloat16 [2, 32, 16, 128, 2048], P(None, 'energy', None, None, 'cell'), may hold values from -0.75 to 0.75
- sigma_lesser: bfloat16 [2, 32, 128, 2048], P(None, 'energy', None, 'cell'), may hold values from -1.5 to 1.5
- w_screened: bfloat16 [2, 32, 16, 128, 2048], P(None, 'energy', None, None, 'cell'), may hold values from -0.75 to 0.75
- coupling: int32 [16, 16], replicated, may hold values 0 or 1
Outputs:
- polarization: bfloat16 [16, 2, 32, 16384], P('cell', None, 'energy')
- w_lesser: bfloat16 [16, 2, 32, 128, 128], P('cell', None, 'energy')
The draws below stay inside these ranges and needn't reach their ends.
Inputs may be any that keep to these rules, and one draw needn't show every extreme that they name: coupling[i, j] is 1 where cell i is coupled to cell j and 0 elsewhere.
All inputs are finite; a program needn't handle non-finite values.
Results may differ from the reference program's by a relative error of at most 0.024.
Values may be sent and summed in bfloat16 or wider, within the bound.
A program may use at most 64 MiB of HBM per device.

```python
import math
import jax
import jax.numpy as jnp
from jax import lax

ORB = 128
CELL_DEV = 1
NCELLS = 16
ENERGIES = 32
N_CELL = 16


def set_ends(values, rng, low, high):
    longest = values.shape.index(max(values.shape))
    spots = []
    for shift in (0, 1):
        where = [jax.random.randint(jax.random.fold_in(rng, axis), (), 0, length) for axis, length in enumerate(values.shape)]
        where[longest] = (where[longest] + shift) % values.shape[longest]
        spots.append(tuple(where))
    return values.at[spots[0]].set(low).at[spots[1]].set(high)


def with_spikes(result, rng, source, target, blocks, factor):
    def block_of(position):
        return (jnp.arange(result.shape[position]) // (result.shape[position] // blocks)).reshape((-1,) + (1,) * (result.ndim - 1 - position))

    one_side = jax.random.permutation(rng, blocks)[block_of(target)]
    second = (block_of(target) + blocks // 2) % blocks
    return jnp.where((block_of(source) == one_side) | (block_of(source) == second), factor * result, result)


def level_of(own_key, shape, shards, least, top_value):
    loudness = 1.0
    for axis_at, shards_of in shards:
        draws = jax.random.uniform(jax.random.fold_in(jax.random.fold_in(own_key, 6), axis_at), (shards_of,), jnp.float32, least / len(shards), top_value / len(shards))
        loudness = loudness * jnp.repeat(jnp.exp(draws), shape[axis_at] // shards_of).reshape((-1,) + (1,) * (len(shape) - 1 - axis_at))
    return loudness


def normal_values(key, dims, width, limit, split=(), held_as=jnp.bfloat16):
    gain = level_of(key, dims, split, -0.22, 0.18) if split else 1.0
    values = jax.random.normal(key, dims, jnp.float32) * width * gain
    return jnp.minimum(jnp.maximum(values, -limit), limit).astype(held_as)


def noise_with(own_key, shape, scale, bound, pieces, heavy, held_as=jnp.bfloat16):
    drawn = scale * jax.random.normal(own_key, shape, jnp.float32)
    if pieces:
        drawn = drawn * level_of(own_key, shape, pieces, -0.22, 0.18)
    return jnp.clip(with_spikes(drawn, jax.random.fold_in(own_key, 3), *heavy), -bound, bound).astype(held_as)


def setup_inputs(seed: int = 0) -> dict:
    key_of = jax.random.split(jax.random.key(seed), 5)
    g_retarded = noise_with(key_of[0], (2, ENERGIES, NCELLS, ORB, NCELLS * ORB), ORB ** -0.5, 0.75, ((1, 32), (4, 16)), (4, 2, 16, 2.0))
    sigma_lesser = normal_values(key_of[1], (2, ENERGIES, ORB, NCELLS * ORB), 0.25, 1.5, ((1, 32), (3, 16)))
    w_screened = noise_with(key_of[2], (2, ENERGIES, NCELLS, ORB, NCELLS * ORB), ORB ** -0.5, 0.75, ((1, 32), (4, 16)), (4, 2, 16, 2.0))
    coupling = set_ends((jax.random.randint(key_of[3], (NCELLS, NCELLS), 0, 2) < 1).astype(jnp.int32), jax.random.fold_in(key_of[3], 1), 0, 1)
    return dict(g_retarded=g_retarded, sigma_lesser=sigma_lesser, w_screened=w_screened, coupling=coupling)


def to_half(value):
    return lax.optimization_barrier(value.astype(jnp.bfloat16)).astype(jnp.float32)

def sandwich(columns, sources, coupling):
    energies = columns.shape[1]
    source = sources.astype(jnp.float32).reshape(2, energies, ORB, NCELLS, ORB)
    src_re = source[0]
    src_im = source[1]
    weights = coupling.astype(jnp.float32)

    def one_row(row_index):
        block = lax.dynamic_index_in_dim(columns, row_index, 2, keepdims=False)
        block = block.astype(jnp.float32).reshape(2, energies, ORB, NCELLS, ORB)
        col_re = block[0]
        col_im = block[1]
        mid_re = jnp.einsum('ebjc,ecjd->ebjd', col_re, src_re) - jnp.einsum('ebjc,ecjd->ebjd', col_im, src_im)
        mid_im = jnp.einsum('ebjc,ecjd->ebjd', col_re, src_im) + jnp.einsum('ebjc,ecjd->ebjd', col_im, src_re)
        mid_re = to_half(mid_re)
        mid_im = to_half(mid_im)
        part_re = jnp.einsum('ebjc,edjc->ejbd', mid_re, col_re) + jnp.einsum('ebjc,edjc->ejbd', mid_im, col_im)
        part_im = jnp.einsum('ebjc,edjc->ejbd', mid_im, col_re) - jnp.einsum('ebjc,edjc->ejbd', mid_re, col_im)
        row_weight = weights[row_index][None, :, None, None]
        part_re = (part_re * row_weight).reshape(energies, N_CELL, CELL_DEV, ORB, ORB).sum(axis=2)
        part_im = (part_im * row_weight).reshape(energies, N_CELL, CELL_DEV, ORB, ORB).sum(axis=2)
        total_re = to_half(part_re).sum(axis=1)
        total_im = to_half(part_im).sum(axis=1)
        return jnp.stack([total_re, total_im], axis=0)
    return lax.map(one_row, jnp.arange(NCELLS, dtype=jnp.int32))

def diagonal_blocks(columns):
    energies = columns.shape[1]

    def one_block(row_index):
        start = (jnp.zeros((), jnp.int32), jnp.zeros((), jnp.int32), row_index, jnp.zeros((), jnp.int32), (row_index * ORB).astype(jnp.int32))
        block = lax.dynamic_slice(columns, start, (2, energies, 1, ORB, ORB))
        return block[:, :, 0].astype(jnp.float32)
    return lax.map(one_block, jnp.arange(NCELLS, dtype=jnp.int32))

def reference(g_retarded, sigma_lesser, w_screened, coupling):
    lesser = sandwich(g_retarded, sigma_lesser, coupling)
    diagonal = diagonal_blocks(g_retarded)
    diag_re = diagonal[:, 0]
    diag_im = diagonal[:, 1]
    greater = lesser + jnp.stack([diag_re - jnp.swapaxes(diag_re, -1, -2), diag_im + jnp.swapaxes(diag_im, -1, -2)], axis=1)
    lesser_half = lesser.astype(jnp.bfloat16).astype(jnp.float32)
    greater_half = greater.astype(jnp.bfloat16).astype(jnp.float32)
    lesser_complex = lesser_half[:, 0] + 1j * lesser_half[:, 1]
    greater_complex = greater_half[:, 0] + 1j * greater_half[:, 1]
    spec_lesser = jnp.fft.fft(lesser_complex, n=2 * ENERGIES, axis=1)
    spec_greater = jnp.fft.fft(greater_complex, n=2 * ENERGIES, axis=1)
    correlation = jnp.fft.ifft(spec_lesser * jnp.conj(spec_greater), axis=1)[:, :ENERGIES]
    polar = -1j / math.sqrt(ENERGIES) * correlation
    polar_half = jnp.stack([jnp.real(polar), jnp.imag(polar)], axis=1).astype(jnp.bfloat16)
    sources = jnp.transpose(polar_half, (1, 2, 3, 0, 4)).reshape(2, ENERGIES, ORB, NCELLS * ORB)
    screened = sandwich(w_screened, sources, coupling)
    polarization = polar_half.reshape(NCELLS, 2, ENERGIES, ORB * ORB)
    return (polarization, screened.astype(jnp.bfloat16))
```

```python
import math

import jax
import jax.numpy as jnp
from jax import lax
from jax.experimental import pallas as pl
from jax.experimental.pallas import tpu as pltpu
from jax.sharding import PartitionSpec as P

ORB = 128
NX = 4
NZ = 4
NE = 32
F32 = jnp.float32
BF16 = jnp.bfloat16
MESH = pl.DeviceIdType.MESH

RIGHT = {("D", 0): 0, ("D", 1): 1, ("N", 2): 2, ("N", 3): 3, ("C", 0): 4, ("C", 1): 5}
LEFT = {("D", 2): 6, ("D", 3): 7, ("N", 0): 8, ("N", 1): 9, ("C", 2): 10, ("C", 3): 11}
UNITS = {**RIGHT, **LEFT}


def dot(a, b):
    return lax.dot_general(a, b, (((1,), (0,)), ((), ())), preferred_element_type=F32)


def dot_t(a, b):
    return lax.dot_general(a, b, (((1,), (1,)), ((), ())), preferred_element_type=F32)


def stacked(re, im):
    top = jnp.concatenate([re, im], axis=1)
    bottom = jnp.concatenate([-im, re], axis=1)
    return jnp.concatenate([top, bottom], axis=0)


def kernel(
    g, s, w, cpl, pol, zout,
    gv, sv, cv, srhs, midv, ub, rb, own, zb, zr, ib, lb, db, lr, dr, a1, a2, br, bi,
    pb, pr, pg, wx, acc, z2b,
    ld, cld, wld, xs, xr, zs, zrs, es, er, ds_, dr_, ps, pr_, ws, wr, gs, gr_, z2s, z2r, pols, lcl,
):
    e = lax.axis_index("energy")
    c = lax.axis_index("cell")
    x = lax.div(c, NZ)
    z = lax.rem(c, NZ)

    def xof(dx):
        return lax.rem(x + dx, NX)

    def zof(dz):
        return lax.rem(z + dz, NZ)

    def cell_of(dx, dz):
        return xof(dx) * NZ + zof(dz)

    def rows_of(dx):
        return pl.ds(xof(dx) * NZ, NZ)

    s_load = pltpu.make_async_copy(s, sv, ld.at[4])
    s_load.start()
    c_load = pltpu.make_async_copy(cpl, cv, cld)
    c_load.start()
    g_load = {}
    for n, dx in enumerate((2, 1, 3, 0)):
        g_load[dx] = pltpu.make_async_copy(g.at[:, rows_of(dx)], gv.at[:, rows_of(dx)], ld.at[n])
        g_load[dx].start()
    w_load = pltpu.make_async_copy(w.at[:, rows_of(0)], wx.at[x], wld)
    w_load.start()

    barrier = pltpu.get_barrier_semaphore()

    @pl.loop(1, NE)
    def _(n):
        pl.semaphore_signal(
            barrier, inc=1, device_id={"energy": lax.rem(e + n, NE)}, device_id_type=MESH
        )

    for d in (1, 2, 3):
        pl.semaphore_signal(barrier, inc=1, device_id={"cell": cell_of(d, 0)}, device_id_type=MESH)
        pl.semaphore_signal(barrier, inc=1, device_id={"cell": cell_of(0, d)}, device_id_type=MESH)

    def to_cell(src, dst, ssem, rsem, dx, dz):
        copy = pltpu.make_async_remote_copy(
            src_ref=src, dst_ref=dst, send_sem=ssem, recv_sem=rsem,
            device_id={"cell": cell_of(dx, dz)}, device_id_type=MESH,
        )
        copy.start()
        return copy

    s_load.wait()
    c_load.wait()
    srhs[...] = stacked(sv[0], sv[1])

    def mids(dx):
        g_load[dx].wait()
        rows = rows_of(dx)
        left = jnp.concatenate(
            [gv[0, rows].reshape(NZ * ORB, ORB), gv[1, rows].reshape(NZ * ORB, ORB)], axis=1
        )
        mid = dot(left, srhs[...])
        for zi in range(NZ):
            weight = cv[xof(dx) * NZ + zi, c].astype(F32)
            midv[dx, zi] = (mid[zi * ORB : (zi + 1) * ORB] * weight).astype(BF16)

    def part(dx, zi):
        i = xof(dx) * NZ + zi
        return dot_t(midv[dx, zi], stacked(gv[0, i], gv[1, i]))

    x_sends = []

    def unit(step, zi):
        u = UNITS[step, zi]
        hop = 1 if (step, zi) in RIGHT else 3
        dest = 2 if step == "D" else hop
        term = part(dest, zi)
        re, im = term[:, :ORB], term[:, ORB:]
        if step == "C":
            d = UNITS["D", zi]
            pltpu.make_async_copy(rb.at[d], rb.at[d], xr.at[d]).wait()
            re = re + rb[d, 0].astype(F32)
            im = im + rb[d, 1].astype(F32)
        ub[u, 0] = re.astype(BF16)
        ub[u, 1] = im.astype(BF16)
        return u, hop

    def send(unit_hop):
        u, hop = unit_hop
        x_sends.append(to_cell(ub.at[u], rb.at[u], xs.at[u], xr.at[u], hop, 0))

    mids(2)
    first = [unit("D", 0), unit("D", 2)]
    pl.semaphore_wait(barrier, NE - 1 + 6)
    for item in first:
        send(item)
    mids(1)
    send(unit("N", 2))
    mids(3)
    send(unit("N", 0))
    send(unit("D", 1))
    send(unit("D", 3))
    send(unit("C", 0))
    send(unit("C", 2))
    send(unit("N", 3))
    send(unit("N", 1))

    def interleaved(re, im, out):
        ib[pl.ds(0, ORB, 2), :] = re
        ib[pl.ds(1, ORB, 2), :] = im
        out[...] = ib[...].reshape(NE, 8, ORB).astype(BF16)

    def spread(src, dst, ssem, rsem):
        dst[e] = src[e]
        for dz in (2, 1, 3, 0):

            @pl.loop(1 if dz == 0 else 0, 8)
            def _(n):
                low = lax.rem(lax.rem(e, 8) + n, 8)
                to = lax.rem(lax.div(e, 8) + dz, 4) * 8 + low
                pltpu.make_async_remote_copy(
                    src_ref=src.at[to], dst_ref=dst.at[e], send_sem=ssem, recv_sem=rsem,
                    device_id={"energy": to}, device_id_type=MESH,
                ).start()

    def arrived(buf, sem):
        part_of = buf.at[pl.ds(0, NE - 1)]
        pltpu.make_async_copy(part_of, part_of, sem).wait()

    g_load[0].wait()
    gr0 = gv[0, c].astype(F32)
    gi0 = gv[1, c].astype(F32)
    interleaved(gr0 - gr0.T, gi0 + gi0.T, db)
    spread(db, dr, ds_, dr_)

    send(unit("C", 1))
    send(unit("C", 3))

    w_sends = []
    for n, dx in enumerate((1, 3, 2)):
        w_sends.append(to_cell(w.at[:, rows_of(dx)], wx.at[x], ws.at[n], wr.at[n], dx, 0))

    rows = rows_of(0)
    left = jnp.concatenate(
        [gv[0, rows].reshape(NZ * ORB, ORB), gv[1, rows].reshape(NZ * ORB, ORB)], axis=1
    )
    mid = dot(left, srhs[...])
    for zi in range(NZ):
        weight = cv[x * NZ + zi, c].astype(F32)
        midv[0, zi] = (mid[zi * ORB : (zi + 1) * ORB] * weight).astype(BF16)
        own[zi] = part(0, zi)

    def x_arrived(u):
        pltpu.make_async_copy(rb.at[u], rb.at[u], xr.at[u]).wait()

    for zi in (0, 2, 1, 3):
        a = UNITS["C", zi]
        b = UNITS["N", zi]
        x_arrived(b)
        x_arrived(a)
        both = own[zi]
        re = both[:, :ORB] + rb[a, 0].astype(F32) + rb[b, 0].astype(F32)
        im = both[:, ORB:] + rb[a, 1].astype(F32) + rb[b, 1].astype(F32)
        own[zi] = jnp.concatenate([re, im], axis=1)
        zb[zi, 0] = re.astype(BF16)
        zb[zi, 1] = im.astype(BF16)

        @pl.when(zi != z)
        def _():
            pltpu.make_async_remote_copy(
                src_ref=zb.at[zi], dst_ref=zr.at[z], send_sem=zs, recv_sem=zrs.at[z],
                device_id={"cell": x * NZ + zi}, device_id_type=MESH,
            ).start()

    both = own[z]
    re, im = both[:, :ORB], both[:, ORB:]
    for dz in (1, 3, 2):
        n = zof(dz)
        pltpu.make_async_copy(zr.at[n], zr.at[n], zrs.at[n]).wait()
        re = re + zr[n, 0].astype(F32)
        im = im + zr[n, 1].astype(F32)

    interleaved(re, im, lb)
    spread(lb, lr, es, er)

    even = lax.rem(lax.broadcasted_iota(jnp.int32, (NE, 8, ORB), 1), 2) == 0

    def row_after(v):
        return pltpu.roll(v, 7, 1)

    def row_before(v):
        return pltpu.roll(v, 1, 1)

    a1[pl.ds(NE, NE)] = jnp.zeros((NE, 8, ORB), F32)
    a2[pl.ds(NE, NE)] = jnp.zeros((NE, 8, ORB), F32)
    arrived(dr, dr_)
    arrived(lr, er)
    low = lr[...].astype(F32)
    high = (low + dr[...].astype(F32)) * (1.0 / math.sqrt(NE))
    a1[pl.ds(0, NE)] = jnp.where(even, row_after(low), -row_before(low))
    a2[pl.ds(0, NE)] = -low
    br[...] = jnp.where(even, high, row_before(high))
    bi[...] = jnp.where(even, row_after(high), high)

    @pl.loop(0, NE)
    def _(shift):
        window = pl.ds(shift, NE)
        pb[shift] = jnp.sum(a1[window] * br[...] + a2[window] * bi[...], axis=0).astype(BF16)

    spread(pb, pr, ps, pr_)

    for n in range(3):
        pltpu.make_async_copy(wx.at[0], wx.at[0], wr.at[n]).wait()
    w_load.wait()

    arrived(pr, pr_)
    g_sends = []
    for n, dx in enumerate((2, 1, 3)):
        g_sends.append(to_cell(pr, pg.at[x], gs.at[n], gr_.at[n], dx, 0))
    pol_out = pltpu.make_async_copy(pr, pol, pols)
    pol_out.start()

    z_sends = []
    recv_of = {2: 0, 3: 1, 1: 2}
    for dx in (0, 1, 3, 2):
        j = xof(dx)
        if dx == 0:
            raw = pr[...]
        else:
            n = recv_of[dx]
            pltpu.make_async_copy(pg.at[j], pg.at[j], gr_.at[n]).wait()
            raw = pg[j]
        ib[...] = raw.astype(F32).reshape(2 * ORB, ORB)
        rhs = stacked(ib[pl.ds(0, ORB, 2), :].astype(BF16), ib[pl.ds(1, ORB, 2), :].astype(BF16))
        left = jnp.concatenate(
            [wx[j, 0].reshape(NZ * ORB, ORB), wx[j, 1].reshape(NZ * ORB, ORB)], axis=1
        )
        mid = dot(left, rhs)
        for zi in range(NZ):
            weight = cv[x * NZ + zi, j * NZ + z].astype(F32)
            midv[dx, zi] = (mid[zi * ORB : (zi + 1) * ORB] * weight).astype(BF16)
        for n, dz in enumerate((2, 1, 3, 0)):
            zi = zof(dz)
            term = dot_t(midv[dx, zi], stacked(wx[j, 0, zi], wx[j, 1, zi]))
            if dx == 0:
                acc[dz] = term
            elif dx != 2:
                acc[dz] += term
            else:
                term = term + acc[dz]
                z2b[dz, 0] = term[:, :ORB].astype(BF16)
                z2b[dz, 1] = term[:, ORB:].astype(BF16)
                if dz == 0:
                    local = pltpu.make_async_copy(z2b.at[0], zout.at[z], lcl)
                    local.start()
                else:
                    z_sends.append(to_cell(z2b.at[dz], zout.at[z], z2s.at[n], z2r.at[n], 0, dz))

    for copy in x_sends + w_sends + g_sends + z_sends:
        copy.wait_send()
    for buf, sem in ((lb, es), (db, ds_), (pb, ps)):
        arrived(buf, sem)
    three = zb.at[pl.ds(0, 3)]
    pltpu.make_async_copy(three, three, zs).wait()
    for n in range(3):
        pltpu.make_async_copy(zout.at[0], zout.at[0], z2r.at[n]).wait()
    pol_out.wait()
    local.wait()


def on_device(g, s, w, coupling):
    block = (2, ORB, ORB)
    dma = pltpu.SemaphoreType.DMA
    vm = pltpu.VMEM
    pol, parts = pl.pallas_call(
        kernel,
        out_shape=(
            jax.ShapeDtypeStruct((NE, 8, ORB), BF16),
            jax.ShapeDtypeStruct((NZ, *block), BF16),
        ),
        in_specs=[pl.BlockSpec(memory_space=pl.ANY)] * 4,
        out_specs=(pl.BlockSpec(memory_space=pl.ANY), pl.BlockSpec(memory_space=pl.ANY)),
        scratch_shapes=[
            vm((2, NX * NZ, ORB, ORB), BF16),
            vm(block, BF16),
            pltpu.SMEM((NX * NZ, NX * NZ), jnp.int32),
            vm((2 * ORB, 2 * ORB), BF16),
            vm((NX, NZ, ORB, 2 * ORB), BF16),
            vm((12, *block), BF16),
            vm((12, *block), BF16),
            vm((NZ, ORB, 2 * ORB), F32),
            vm((NZ, *block), BF16),
            vm((NZ, *block), BF16),
            vm((2 * ORB, ORB), F32),
            vm((NE, 8, ORB), BF16),
            vm((NE, 8, ORB), BF16),
            vm((NE, 8, ORB), BF16),
            vm((NE, 8, ORB), BF16),
            vm((2 * NE, 8, ORB), F32),
            vm((2 * NE, 8, ORB), F32),
            vm((NE, 8, ORB), F32),
            vm((NE, 8, ORB), F32),
            vm((NE, 8, ORB), BF16),
            vm((NE, 8, ORB), BF16),
            vm((NX, NE, 8, ORB), BF16),
            vm((NX, 2, NZ, ORB, ORB), BF16),
            vm((NZ, ORB, 2 * ORB), F32),
            vm((NZ, *block), BF16),
            dma((5,)),
            dma,
            dma,
            dma((12,)),
            dma((12,)),
            dma,
            dma((NZ,)),
            dma,
            dma,
            dma,
            dma,
            dma,
            dma,
            dma((3,)),
            dma((3,)),
            dma((3,)),
            dma((3,)),
            dma((3,)),
            dma((3,)),
            dma,
            dma,
        ],
        compiler_params=pltpu.CompilerParams(collective_id=0, has_side_effects=True),
    )(g.reshape(2, NX * NZ, ORB, ORB), s.reshape(block), w.reshape(2, NX * NZ, ORB, ORB), coupling)
    polar = jnp.transpose(pol.reshape(ORB, 2, ORB), (1, 0, 2)).reshape(1, 2, 1, ORB * ORB)
    screened = parts.astype(F32).sum(axis=0).astype(BF16)
    return polar, screened.reshape(1, 2, 1, ORB, ORB)


def solution(mesh):
    return jax.shard_map(
        on_device,
        mesh=mesh,
        in_specs=(
            P(None, "energy", None, None, "cell"),
            P(None, "energy", None, "cell"),
            P(None, "energy", None, None, "cell"),
            P(),
        ),
        out_specs=(P("cell", None, "energy", None), P("cell", None, "energy", None, None)),
        check_vma=False,
    )
```

```python
import math

import jax
import jax.numpy as jnp
from jax import lax
from jax.experimental import pallas as pl
from jax.experimental.pallas import tpu as pltpu
from jax.sharding import PartitionSpec as P

ORB = 128
NX = 4
NZ = 4
NE = 32
F32 = jnp.float32
BF16 = jnp.bfloat16
MESH = pl.DeviceIdType.MESH

RIGHT = {("D", 0): 0, ("D", 1): 1, ("N", 2): 2, ("N", 3): 3, ("C", 0): 4, ("C", 1): 5}
LEFT = {("D", 2): 6, ("D", 3): 7, ("N", 0): 8, ("N", 1): 9, ("C", 2): 10, ("C", 3): 11}
UNITS = {**RIGHT, **LEFT}


def dot(a, b):
    return lax.dot_general(a, b, (((1,), (0,)), ((), ())), preferred_element_type=F32)


def dot_t(a, b):
    return lax.dot_general(a, b, (((1,), (1,)), ((), ())), preferred_element_type=F32)


def stacked(re, im):
    top = jnp.concatenate([re, im], axis=1)
    bottom = jnp.concatenate([-im, re], axis=1)
    return jnp.concatenate([top, bottom], axis=0)


def kernel(
    g, s, w, cpl, pol, zout,
    gv, sv, cv, srhs, midv, ub, rb, own, zb, zr, ib, lb, db, lr, dr, a1, a2, br, bi,
    pb, pr, pg, wx, acc, z2b,
    ld, cld, wld, xs, xr, zs, zrs, es, er, ds_, dr_, ps, pr_, f1, f2, ws, wr, gs, gr_, z2s, z2r, pols, lcl,
):
    e = lax.axis_index("energy")
    c = lax.axis_index("cell")
    x = lax.div(c, NZ)
    z = lax.rem(c, NZ)

    def xof(dx):
        return lax.rem(x + dx, NX)

    def zof(dz):
        return lax.rem(z + dz, NZ)

    def cell_of(dx, dz):
        return xof(dx) * NZ + zof(dz)

    def rows_of(dx):
        return pl.ds(xof(dx) * NZ, NZ)

    s_load = pltpu.make_async_copy(s, sv, ld.at[4])
    s_load.start()
    c_load = pltpu.make_async_copy(cpl, cv, cld)
    c_load.start()
    g_load = {}
    for n, dx in enumerate((2, 1, 3, 0)):
        g_load[dx] = pltpu.make_async_copy(g.at[:, rows_of(dx)], gv.at[:, rows_of(dx)], ld.at[n])
        g_load[dx].start()
    w_load = pltpu.make_async_copy(w.at[:, rows_of(0)], wx.at[x], wld)
    w_load.start()

    barrier = pltpu.get_barrier_semaphore()

    plane = lax.div(e, 8) * 8

    @pl.loop(1, 8)
    def _(n):
        mate = plane + lax.rem(e + n, 8)
        pl.semaphore_signal(barrier, inc=1, device_id={"energy": mate}, device_id_type=MESH)

    def greet_along_z(sem):
        for d in (8, NE - 8):
            pl.semaphore_signal(
                sem, inc=1, device_id={"energy": lax.rem(e + d, NE)}, device_id_type=MESH
            )

    greet_along_z(barrier)
    for d in (1, 2, 3):
        pl.semaphore_signal(barrier, inc=1, device_id={"cell": cell_of(d, 0)}, device_id_type=MESH)
        pl.semaphore_signal(barrier, inc=1, device_id={"cell": cell_of(0, d)}, device_id_type=MESH)

    def to_cell(src, dst, ssem, rsem, dx, dz):
        copy = pltpu.make_async_remote_copy(
            src_ref=src, dst_ref=dst, send_sem=ssem, recv_sem=rsem,
            device_id={"cell": cell_of(dx, dz)}, device_id_type=MESH,
        )
        copy.start()
        return copy

    s_load.wait()
    c_load.wait()
    srhs[...] = stacked(sv[0], sv[1])

    def mids(dx):
        g_load[dx].wait()
        rows = rows_of(dx)
        left = jnp.concatenate(
            [gv[0, rows].reshape(NZ * ORB, ORB), gv[1, rows].reshape(NZ * ORB, ORB)], axis=1
        )
        mid = dot(left, srhs[...])
        for zi in range(NZ):
            weight = cv[xof(dx) * NZ + zi, c].astype(F32)
            midv[dx, zi] = (mid[zi * ORB : (zi + 1) * ORB] * weight).astype(BF16)

    def part(dx, zi):
        i = xof(dx) * NZ + zi
        return dot_t(midv[dx, zi], stacked(gv[0, i], gv[1, i]))

    x_sends = []

    def unit(step, zi):
        u = UNITS[step, zi]
        hop = 1 if (step, zi) in RIGHT else 3
        dest = 2 if step == "D" else hop
        term = part(dest, zi)
        re, im = term[:, :ORB], term[:, ORB:]
        if step == "C":
            d = UNITS["D", zi]
            pltpu.make_async_copy(rb.at[d], rb.at[d], xr.at[d]).wait()
            re = re + rb[d, 0].astype(F32)
            im = im + rb[d, 1].astype(F32)
        ub[u, 0] = re.astype(BF16)
        ub[u, 1] = im.astype(BF16)
        return u, hop

    def send(unit_hop):
        u, hop = unit_hop
        x_sends.append(to_cell(ub.at[u], rb.at[u], xs.at[u], xr.at[u], hop, 0))

    mids(2)
    first = [unit("D", 0), unit("D", 2)]
    pl.semaphore_wait(barrier, 7 + 2 + 6)
    greet_along_z(f1)
    for item in first:
        send(item)
    mids(1)
    send(unit("N", 2))
    mids(3)
    send(unit("N", 0))
    send(unit("D", 1))
    send(unit("D", 3))
    send(unit("C", 0))
    send(unit("C", 2))
    send(unit("N", 3))
    send(unit("N", 1))

    def interleaved(re, im, out):
        ib[pl.ds(0, ORB, 2), :] = re
        ib[pl.ds(1, ORB, 2), :] = im
        out[...] = ib[...].reshape(NE, 8, ORB).astype(BF16)

    def send_plane(src, dst, ssem, rsem, dz):
        @pl.loop(1 if dz == 0 else 0, 8)
        def _(n):
            to = lax.rem(plane + 8 * dz, NE) + lax.rem(e + n, 8)
            pltpu.make_async_remote_copy(
                src_ref=src.at[to], dst_ref=dst.at[e], send_sem=ssem, recv_sem=rsem,
                device_id={"energy": to}, device_id_type=MESH,
            ).start()

    def spread(src, dst, ssem, rsem):
        dst[e] = src[e]
        for dz in (2, 1, 3, 0):
            send_plane(src, dst, ssem, rsem, dz)

    def arrived(buf, sem):
        part_of = buf.at[pl.ds(0, NE - 1)]
        pltpu.make_async_copy(part_of, part_of, sem).wait()

    g_load[0].wait()
    gr0 = gv[0, c].astype(F32)
    gi0 = gv[1, c].astype(F32)
    interleaved(gr0 - gr0.T, gi0 + gi0.T, db)
    pl.semaphore_wait(f1, 2)
    greet_along_z(f2)

    send(unit("C", 1))
    send(unit("C", 3))

    w_sends = []
    for n, dx in enumerate((1, 3, 2)):
        w_sends.append(to_cell(w.at[:, rows_of(dx)], wx.at[x], ws.at[n], wr.at[n], dx, 0))

    rows = rows_of(0)
    left = jnp.concatenate(
        [gv[0, rows].reshape(NZ * ORB, ORB), gv[1, rows].reshape(NZ * ORB, ORB)], axis=1
    )
    mid = dot(left, srhs[...])
    for zi in range(NZ):
        weight = cv[x * NZ + zi, c].astype(F32)
        midv[0, zi] = (mid[zi * ORB : (zi + 1) * ORB] * weight).astype(BF16)
        own[zi] = part(0, zi)

    pl.semaphore_wait(f2, 2)
    spread(db, dr, ds_, dr_)

    def x_arrived(u):
        pltpu.make_async_copy(rb.at[u], rb.at[u], xr.at[u]).wait()

    for zi in (0, 2, 1, 3):
        a = UNITS["C", zi]
        b = UNITS["N", zi]
        x_arrived(b)
        x_arrived(a)
        both = own[zi]
        re = both[:, :ORB] + rb[a, 0].astype(F32) + rb[b, 0].astype(F32)
        im = both[:, ORB:] + rb[a, 1].astype(F32) + rb[b, 1].astype(F32)
        own[zi] = jnp.concatenate([re, im], axis=1)
        zb[zi, 0] = re.astype(BF16)
        zb[zi, 1] = im.astype(BF16)

        @pl.when(zi != z)
        def _():
            pltpu.make_async_remote_copy(
                src_ref=zb.at[zi], dst_ref=zr.at[z], send_sem=zs, recv_sem=zrs.at[z],
                device_id={"cell": x * NZ + zi}, device_id_type=MESH,
            ).start()

    both = own[z]
    re, im = both[:, :ORB], both[:, ORB:]
    for dz in (1, 3, 2):
        n = zof(dz)
        pltpu.make_async_copy(zr.at[n], zr.at[n], zrs.at[n]).wait()
        re = re + zr[n, 0].astype(F32)
        im = im + zr[n, 1].astype(F32)

    interleaved(re, im, lb)
    spread(lb, lr, es, er)

    even = lax.rem(lax.broadcasted_iota(jnp.int32, (NE, 8, ORB), 1), 2) == 0

    def row_after(v):
        return pltpu.roll(v, 7, 1)

    def row_before(v):
        return pltpu.roll(v, 1, 1)

    a1[pl.ds(NE, 8)] = jnp.zeros((8, 8, ORB), F32)
    a2[pl.ds(NE, 8)] = jnp.zeros((8, 8, ORB), F32)
    arrived(dr, dr_)
    arrived(lr, er)
    low = lr[...].astype(F32)
    high = (low + dr[...].astype(F32)) * (1.0 / math.sqrt(NE))
    a1[pl.ds(0, NE)] = jnp.where(even, row_after(low), -row_before(low))
    a2[pl.ds(0, NE)] = -low
    br[...] = jnp.where(even, high, row_before(high))
    bi[...] = jnp.where(even, row_after(high), high)

    for dz in (2, 1, 3, 0):
        first = lax.rem(plane + 8 * dz, NE)

        def eight(block, total, first=first):
            for n in range(8):
                at = block * 8 + n
                window = pl.ds(first + at, 8)
                total = total + a1[window] * br[at] + a2[window] * bi[at]
            return total

        total = lax.fori_loop(0, lax.div(NE - first, 8), eight, jnp.zeros((8, 8, ORB), F32))
        pb[pl.ds(first, 8)] = total.astype(BF16)
        if dz == 0:
            pr[e] = pb[e]
        send_plane(pb, pr, ps, pr_.at[dz], dz)

    for n in range(3):
        pltpu.make_async_copy(wx.at[0], wx.at[0], wr.at[n]).wait()
    w_load.wait()

    g_sends = []
    for dz in (0, 1, 3, 2):
        tiles = pl.ds(lax.rem(plane + (NE - 8 * dz), NE), 8)
        came = pr.at[pl.ds(0, 7 if dz == 0 else 8)]
        pltpu.make_async_copy(came, came, pr_.at[dz]).wait()
        for n, dx in enumerate((2, 1, 3)):
            g_sends.append(to_cell(pr.at[tiles], pg.at[x, tiles], gs.at[n], gr_.at[n], dx, 0))
    pol_out = pltpu.make_async_copy(pr, pol, pols)
    pol_out.start()

    z_sends = []
    recv_of = {2: 0, 3: 1, 1: 2}
    for dx in (0, 1, 3, 2):
        j = xof(dx)
        if dx == 0:
            raw = pr[...]
        else:
            n = recv_of[dx]
            pltpu.make_async_copy(pg.at[j], pg.at[j], gr_.at[n]).wait()
            raw = pg[j]
        ib[...] = raw.astype(F32).reshape(2 * ORB, ORB)
        rhs = stacked(ib[pl.ds(0, ORB, 2), :].astype(BF16), ib[pl.ds(1, ORB, 2), :].astype(BF16))
        left = jnp.concatenate(
            [wx[j, 0].reshape(NZ * ORB, ORB), wx[j, 1].reshape(NZ * ORB, ORB)], axis=1
        )
        mid = dot(left, rhs)
        for zi in range(NZ):
            weight = cv[x * NZ + zi, j * NZ + z].astype(F32)
            midv[dx, zi] = (mid[zi * ORB : (zi + 1) * ORB] * weight).astype(BF16)
        for n, dz in enumerate((2, 3, 1, 0)):
            zi = lax.bitwise_xor(z, dz)
            term = dot_t(midv[dx, zi], stacked(wx[j, 0, zi], wx[j, 1, zi]))
            if dx == 0:
                acc[dz] = term
            elif dx != 2:
                acc[dz] += term
            else:
                term = term + acc[dz]
                z2b[dz, 0] = term[:, :ORB].astype(BF16)
                z2b[dz, 1] = term[:, ORB:].astype(BF16)
                if dz == 0:
                    local = pltpu.make_async_copy(z2b.at[0], zout.at[z], lcl)
                    local.start()
                else:
                    copy = pltpu.make_async_remote_copy(
                        src_ref=z2b.at[dz], dst_ref=zout.at[z], send_sem=z2s.at[n], recv_sem=z2r.at[n],
                        device_id={"cell": x * NZ + zi}, device_id_type=MESH,
                    )
                    copy.start()
                    z_sends.append(copy)

    for copy in x_sends + w_sends + g_sends + z_sends:
        copy.wait_send()
    for buf, sem in ((lb, es), (db, ds_), (pb, ps)):
        arrived(buf, sem)
    three = zb.at[pl.ds(0, 3)]
    pltpu.make_async_copy(three, three, zs).wait()
    for n in range(3):
        pltpu.make_async_copy(zout.at[0], zout.at[0], z2r.at[n]).wait()
    pol_out.wait()
    local.wait()


def on_device(g, s, w, coupling):
    block = (2, ORB, ORB)
    dma = pltpu.SemaphoreType.DMA
    vm = pltpu.VMEM
    pol, parts = pl.pallas_call(
        kernel,
        out_shape=(
            jax.ShapeDtypeStruct((NE, 8, ORB), BF16),
            jax.ShapeDtypeStruct((NZ, *block), BF16),
        ),
        in_specs=[pl.BlockSpec(memory_space=pl.ANY)] * 4,
        out_specs=(pl.BlockSpec(memory_space=pl.ANY), pl.BlockSpec(memory_space=pl.ANY)),
        scratch_shapes=[
            vm((2, NX * NZ, ORB, ORB), BF16),
            vm(block, BF16),
            pltpu.SMEM((NX * NZ, NX * NZ), jnp.int32),
            vm((2 * ORB, 2 * ORB), BF16),
            vm((NX, NZ, ORB, 2 * ORB), BF16),
            vm((12, *block), BF16),
            vm((12, *block), BF16),
            vm((NZ, ORB, 2 * ORB), F32),
            vm((NZ, *block), BF16),
            vm((NZ, *block), BF16),
            vm((2 * ORB, ORB), F32),
            vm((NE, 8, ORB), BF16),
            vm((NE, 8, ORB), BF16),
            vm((NE, 8, ORB), BF16),
            vm((NE, 8, ORB), BF16),
            vm((NE + 8, 8, ORB), F32),
            vm((NE + 8, 8, ORB), F32),
            vm((NE, 8, ORB), F32),
            vm((NE, 8, ORB), F32),
            vm((NE, 8, ORB), BF16),
            vm((NE, 8, ORB), BF16),
            vm((NX, NE, 8, ORB), BF16),
            vm((NX, 2, NZ, ORB, ORB), BF16),
            vm((NZ, ORB, 2 * ORB), F32),
            vm((NZ, *block), BF16),
            dma((5,)),
            dma,
            dma,
            dma((12,)),
            dma((12,)),
            dma,
            dma((NZ,)),
            dma,
            dma,
            dma,
            dma,
            dma,
            dma((4,)),
            pltpu.SemaphoreType.REGULAR,
            pltpu.SemaphoreType.REGULAR,
            dma((3,)),
            dma((3,)),
            dma((3,)),
            dma((3,)),
            dma((3,)),
            dma((3,)),
            dma,
            dma,
        ],
        compiler_params=pltpu.CompilerParams(collective_id=0, has_side_effects=True),
    )(g.reshape(2, NX * NZ, ORB, ORB), s.reshape(block), w.reshape(2, NX * NZ, ORB, ORB), coupling)
    polar = jnp.transpose(pol.reshape(ORB, 2, ORB), (1, 0, 2)).reshape(1, 2, 1, ORB * ORB)
    screened = sum(parts[n].astype(F32) for n in range(NZ)).astype(BF16)
    return polar, screened.reshape(1, 2, 1, ORB, ORB)


def solution(mesh):
    return jax.shard_map(
        on_device,
        mesh=mesh,
        in_specs=(
            P(None, "energy", None, None, "cell"),
            P(None, "energy", None, "cell"),
            P(None, "energy", None, None, "cell"),
            P(),
        ),
        out_specs=(P("cell", None, "energy", None), P("cell", None, "energy", None, None)),
        check_vma=False,
    )
```

```python
import math

import jax
import jax.numpy as jnp
from jax import lax
from jax.experimental import pallas as pl
from jax.experimental.pallas import tpu as pltpu
from jax.sharding import PartitionSpec as P

ORB = 128
NX = 4
NZ = 4
NE = 32
F32 = jnp.float32
BF16 = jnp.bfloat16
MESH = pl.DeviceIdType.MESH
VL = 16 * 1024 * 1024

RIGHT = {("D", 0): 0, ("D", 1): 1, ("N", 2): 2, ("N", 3): 3, ("C", 0): 4, ("C", 1): 5}
LEFT = {("D", 2): 6, ("D", 3): 7, ("N", 0): 8, ("N", 1): 9, ("C", 2): 10, ("C", 3): 11}
UNITS = {**RIGHT, **LEFT}


def dot(a, b):
    return lax.dot_general(a, b, (((1,), (0,)), ((), ())), preferred_element_type=F32)


def dot_t(a, b):
    return lax.dot_general(a, b, (((1,), (1,)), ((), ())), preferred_element_type=F32)


def stacked(re, im):
    top = jnp.concatenate([re, im], axis=1)
    bottom = jnp.concatenate([-im, re], axis=1)
    return jnp.concatenate([top, bottom], axis=0)


def kernel(
    g, s, w, cpl, pol, zout,
    gv, sv, cv, srhs, midv, ub, rb, own, zb, zr, ib, lb, db, lr, a1, a2, br, bi,
    pb, pr, pg, wx, acc, z2b,
    ld, cld, wld, xs, xr, zs, zrs, es, er, ps, pr_, fr, f1, f2, ws, wr, gs, gr_, z2s, z2r, pols, lcl,
):
    e = lax.axis_index("energy")
    c = lax.axis_index("cell")
    x = lax.div(c, NZ)
    z = lax.rem(c, NZ)

    def xof(dx):
        return lax.rem(x + dx, NX)

    def zof(dz):
        return lax.rem(z + dz, NZ)

    def cell_of(dx, dz):
        return xof(dx) * NZ + zof(dz)

    def rows_of(dx):
        return pl.ds(xof(dx) * NZ, NZ)

    s_load = pltpu.make_async_copy(s, sv, ld.at[4])
    s_load.start()
    c_load = pltpu.make_async_copy(cpl, cv, cld)
    c_load.start()
    g_load = {}
    for n, dx in enumerate((2, 1, 3, 0)):
        g_load[dx] = pltpu.make_async_copy(g.at[:, rows_of(dx)], gv.at[:, rows_of(dx)], ld.at[n])
        g_load[dx].start()
    w_load = pltpu.make_async_copy(w.at[:, rows_of(0)], wx.at[x], wld)
    w_load.start()

    barrier = pltpu.get_barrier_semaphore()

    plane = lax.div(e, 8) * 8
    seat = lax.rem(e, 8)

    def greet(sem):
        for d in (1, NX - 1):
            pl.semaphore_signal(sem, inc=1, device_id={"cell": cell_of(d, 0)}, device_id_type=MESH)
        for d in (2, 6):
            to = plane + lax.rem(seat + d, 8)
            pl.semaphore_signal(sem, inc=1, device_id={"energy": to}, device_id_type=MESH)
        mate = lax.bitwise_xor(e, 1)
        pl.semaphore_signal(sem, inc=1, device_id={"energy": mate}, device_id_type=MESH)
        for d in (1, 15):
            at = lax.rem(lax.div(e, 8) * NZ + z + d, 16)
            to = {"energy": lax.div(at, NZ) * 8 + seat, "cell": x * NZ + lax.rem(at, NZ)}
            pl.semaphore_signal(sem, inc=1, device_id=to, device_id_type=MESH)

    def greet_along_z(sem):
        for d in (8, NE - 8):
            pl.semaphore_signal(
                sem, inc=1, device_id={"energy": lax.rem(e + d, NE)}, device_id_type=MESH
            )

    def heard(sem, count):
        pl.semaphore_wait(sem, count)

    greet(barrier)

    def to_cell(src, dst, ssem, rsem, dx, dz):
        copy = pltpu.make_async_remote_copy(
            src_ref=src, dst_ref=dst, send_sem=ssem, recv_sem=rsem,
            device_id={"cell": cell_of(dx, dz)}, device_id_type=MESH,
        )
        copy.start()
        return copy

    s_load.wait()
    c_load.wait()
    srhs[...] = stacked(sv[0], sv[1])

    def mids(dx):
        g_load[dx].wait()
        rows = rows_of(dx)
        left = jnp.concatenate(
            [gv[0, rows].reshape(NZ * ORB, ORB), gv[1, rows].reshape(NZ * ORB, ORB)], axis=1
        )
        mid = dot(left, srhs[...])
        for zi in range(NZ):
            weight = cv[xof(dx) * NZ + zi, c].astype(F32)
            midv[dx, zi] = (mid[zi * ORB : (zi + 1) * ORB] * weight).astype(BF16)

    def part(dx, zi):
        i = xof(dx) * NZ + zi
        return dot_t(midv[dx, zi], stacked(gv[0, i], gv[1, i]))

    x_sends = []

    def unit(step, zi):
        u = UNITS[step, zi]
        hop = 1 if (step, zi) in RIGHT else 3
        dest = 2 if step == "D" else hop
        term = part(dest, zi)
        re, im = term[:, :ORB], term[:, ORB:]
        if step == "C":
            d = UNITS["D", zi]
            pltpu.make_async_copy(rb.at[d], rb.at[d], xr.at[d]).wait()
            re = re + rb[d, 0].astype(F32)
            im = im + rb[d, 1].astype(F32)
        ub[u, 0] = re.astype(BF16)
        ub[u, 1] = im.astype(BF16)
        return u, hop

    def send(unit_hop):
        u, hop = unit_hop
        x_sends.append(to_cell(ub.at[u], rb.at[u], xs.at[u], xr.at[u], hop, 0))

    mids(2)
    first = [unit("D", 0), unit("D", 2)]
    heard(barrier, 7)
    greet(fr.at[0])
    for item in first:
        send(item)
    mids(1)
    send(unit("N", 2))
    mids(3)
    send(unit("N", 0))
    heard(fr.at[0], 7)
    greet(fr.at[1])
    send(unit("D", 1))
    send(unit("D", 3))
    heard(fr.at[1], 7)
    greet(fr.at[2])
    send(unit("C", 0))
    send(unit("C", 2))
    send(unit("N", 3))
    send(unit("N", 1))
    heard(fr.at[2], 7)
    greet_along_z(f1)

    def interleaved(re, im, out):
        out[pl.ds(0, ORB, 2), :] = re
        out[pl.ds(1, ORB, 2), :] = im

    def send_plane(src, dst, ssem, rsem, dz):
        @pl.loop(1 if dz == 0 else 0, 8)
        def _(n):
            to = lax.rem(plane + 8 * dz, NE) + lax.rem(e + n, 8)
            pltpu.make_async_remote_copy(
                src_ref=src.at[to], dst_ref=dst.at[e], send_sem=ssem, recv_sem=rsem,
                device_id={"energy": to}, device_id_type=MESH,
            ).start()

    def arrived(buf, sem):
        part_of = buf.at[pl.ds(0, NE - 1)]
        pltpu.make_async_copy(part_of, part_of, sem).wait()

    send(unit("C", 1))
    send(unit("C", 3))

    w_sends = []
    for n, dx in enumerate((1, 3, 2)):
        w_sends.append(to_cell(w.at[:, rows_of(dx)], wx.at[x], ws.at[n], wr.at[n], dx, 0))

    mids(0)
    for zi in range(NZ):
        own[zi] = part(0, zi)
    gr0 = gv[0, c].astype(F32)
    gi0 = gv[1, c].astype(F32)
    interleaved(gr0 - gr0.T, gi0 + gi0.T, db)
    heard(f1, 2)
    greet_along_z(f2)

    def x_arrived(u):
        pltpu.make_async_copy(rb.at[u], rb.at[u], xr.at[u]).wait()

    for zi in (0, 2, 1, 3):
        a = UNITS["C", zi]
        b = UNITS["N", zi]
        x_arrived(b)
        x_arrived(a)
        both = own[zi]
        re = both[:, :ORB] + rb[a, 0].astype(F32) + rb[b, 0].astype(F32)
        im = both[:, ORB:] + rb[a, 1].astype(F32) + rb[b, 1].astype(F32)
        own[zi] = jnp.concatenate([re, im], axis=1)
        zb[zi, 0] = re.astype(BF16)
        zb[zi, 1] = im.astype(BF16)

        @pl.when(zi != z)
        def _():
            pltpu.make_async_remote_copy(
                src_ref=zb.at[zi], dst_ref=zr.at[z], send_sem=zs, recv_sem=zrs.at[z],
                device_id={"cell": x * NZ + zi}, device_id_type=MESH,
            ).start()

    both = own[z]
    re, im = both[:, :ORB], both[:, ORB:]
    for dz in (1, 3, 2):
        n = zof(dz)
        pltpu.make_async_copy(zr.at[n], zr.at[n], zrs.at[n]).wait()
        re = re + zr[n, 0].astype(F32)
        im = im + zr[n, 1].astype(F32)

    interleaved(re, im, ib)
    lb[:, 0] = ib[...].reshape(NE, 8, ORB).astype(BF16)
    lb[:, 1] = (ib[...] + db[...]).reshape(NE, 8, ORB).astype(BF16)
    heard(f2, 2)
    lr[e] = lb[e]
    for dz in (2, 1, 3, 0):
        send_plane(lb, lr, es, er, dz)

    even = lax.rem(lax.broadcasted_iota(jnp.int32, (NE, 8, ORB), 1), 2) == 0

    def row_after(v):
        return pltpu.roll(v, 7, 1)

    def row_before(v):
        return pltpu.roll(v, 1, 1)

    a1[pl.ds(NE, 8)] = jnp.zeros((8, 8, ORB), F32)
    a2[pl.ds(NE, 8)] = jnp.zeros((8, 8, ORB), F32)
    arrived(lr, er)
    low = lr[:, 0].astype(F32)
    high = lr[:, 1].astype(F32) * (1.0 / math.sqrt(NE))
    a1[pl.ds(0, NE)] = jnp.where(even, row_after(low), -row_before(low))
    a2[pl.ds(0, NE)] = -low
    br[...] = jnp.where(even, high, row_before(high))
    bi[...] = jnp.where(even, row_after(high), high)

    for dz in (2, 1, 3, 0):
        first = lax.rem(plane + 8 * dz, NE)

        def eight(block, total, first=first):
            for n in range(8):
                at = block * 8 + n
                window = pl.ds(first + at, 8)
                total = total + a1[window] * br[at] + a2[window] * bi[at]
            return total

        total = lax.fori_loop(0, lax.div(NE - first, 8), eight, jnp.zeros((8, 8, ORB), F32))
        pb[pl.ds(first, 8)] = total.astype(BF16)
        if dz == 0:
            pr[e] = pb[e]
        send_plane(pb, pr, ps, pr_.at[dz], dz)

    for n in range(3):
        pltpu.make_async_copy(wx.at[0], wx.at[0], wr.at[n]).wait()
    w_load.wait()

    g_sends = []
    for dz in (0, 1, 3, 2):
        tiles = pl.ds(lax.rem(plane + (NE - 8 * dz), NE), 8)
        came = pr.at[pl.ds(0, 7 if dz == 0 else 8)]
        pltpu.make_async_copy(came, came, pr_.at[dz]).wait()
        for n, dx in enumerate((2, 1, 3)):
            g_sends.append(to_cell(pr.at[tiles], pg.at[x, tiles], gs.at[n], gr_.at[n], dx, 0))
    pol_out = pltpu.make_async_copy(pr, pol, pols)
    pol_out.start()

    z_sends = []
    recv_of = {2: 0, 3: 1, 1: 2}
    for dx in (0, 1, 3, 2):
        j = xof(dx)
        if dx == 0:
            raw = pr[...]
        else:
            n = recv_of[dx]
            pltpu.make_async_copy(pg.at[j], pg.at[j], gr_.at[n]).wait()
            raw = pg[j]
        ib[...] = raw.astype(F32).reshape(2 * ORB, ORB)
        rhs = stacked(ib[pl.ds(0, ORB, 2), :].astype(BF16), ib[pl.ds(1, ORB, 2), :].astype(BF16))
        left = jnp.concatenate(
            [wx[j, 0].reshape(NZ * ORB, ORB), wx[j, 1].reshape(NZ * ORB, ORB)], axis=1
        )
        mid = dot(left, rhs)
        for zi in range(NZ):
            weight = cv[x * NZ + zi, j * NZ + z].astype(F32)
            midv[dx, zi] = (mid[zi * ORB : (zi + 1) * ORB] * weight).astype(BF16)
        for n, dz in enumerate((2, 3, 1, 0)):
            zi = lax.bitwise_xor(z, dz)
            term = dot_t(midv[dx, zi], stacked(wx[j, 0, zi], wx[j, 1, zi]))
            if dx == 0:
                acc[dz] = term
            elif dx != 2:
                acc[dz] += term
            else:
                term = term + acc[dz]
                z2b[dz, 0] = term[:, :ORB].astype(BF16)
                z2b[dz, 1] = term[:, ORB:].astype(BF16)
                if dz == 0:
                    local = pltpu.make_async_copy(z2b.at[0], zout.at[z], lcl)
                    local.start()
                else:
                    copy = pltpu.make_async_remote_copy(
                        src_ref=z2b.at[dz], dst_ref=zout.at[z], send_sem=z2s.at[n], recv_sem=z2r.at[n],
                        device_id={"cell": x * NZ + zi}, device_id_type=MESH,
                    )
                    copy.start()
                    z_sends.append(copy)

    for copy in x_sends + w_sends + g_sends + z_sends:
        copy.wait_send()
    for buf, sem in ((lb, es), (pb, ps)):
        arrived(buf, sem)
    three = zb.at[pl.ds(0, 3)]
    pltpu.make_async_copy(three, three, zs).wait()
    for n in range(3):
        pltpu.make_async_copy(zout.at[0], zout.at[0], z2r.at[n]).wait()
    pol_out.wait()
    local.wait()


def on_device(g, s, w, coupling):
    block = (2, ORB, ORB)
    dma = pltpu.SemaphoreType.DMA
    vm = pltpu.VMEM
    operands = (
        g.reshape(2, NX * NZ, ORB, ORB), s.reshape(block), w.reshape(2, NX * NZ, ORB, ORB), coupling
    )
    pol, parts = pl.pallas_call(
        kernel,
        out_shape=(
            jax.ShapeDtypeStruct((NE, 8, ORB), BF16),
            jax.ShapeDtypeStruct((NZ, *block), BF16),
        ),
        in_specs=[pl.BlockSpec(memory_space=pltpu.HBM)] * 4,
        out_specs=(pl.BlockSpec(memory_space=pl.ANY), pl.BlockSpec(memory_space=pl.ANY)),
        scratch_shapes=[
            vm((2, NX * NZ, ORB, ORB), BF16),
            vm(block, BF16),
            pltpu.SMEM((NX * NZ, NX * NZ), jnp.int32),
            vm((2 * ORB, 2 * ORB), BF16),
            vm((NX, NZ, ORB, 2 * ORB), BF16),
            vm((12, *block), BF16),
            vm((12, *block), BF16),
            vm((NZ, ORB, 2 * ORB), F32),
            vm((NZ, *block), BF16),
            vm((NZ, *block), BF16),
            vm((2 * ORB, ORB), F32),
            vm((NE, 2, 8, ORB), BF16),
            vm((2 * ORB, ORB), F32),
            vm((NE, 2, 8, ORB), BF16),
            vm((NE + 8, 8, ORB), F32),
            vm((NE + 8, 8, ORB), F32),
            vm((NE, 8, ORB), F32),
            vm((NE, 8, ORB), F32),
            vm((NE, 8, ORB), BF16),
            vm((NE, 8, ORB), BF16),
            vm((NX, NE, 8, ORB), BF16),
            vm((NX, 2, NZ, ORB, ORB), BF16),
            vm((NZ, ORB, 2 * ORB), F32),
            vm((NZ, *block), BF16),
            dma((5,)),
            dma,
            dma,
            dma((12,)),
            dma((12,)),
            dma,
            dma((NZ,)),
            dma,
            dma,
            dma,
            dma((4,)),
            pltpu.SemaphoreType.REGULAR((3,)),
            pltpu.SemaphoreType.REGULAR,
            pltpu.SemaphoreType.REGULAR,
            dma((3,)),
            dma((3,)),
            dma((3,)),
            dma((3,)),
            dma((3,)),
            dma((3,)),
            dma,
            dma,
        ],
        compiler_params=pltpu.CompilerParams(collective_id=0, has_side_effects=True, vmem_limit_bytes=VL),
    )(*(pltpu.with_memory_space_constraint(v, pltpu.HBM) for v in operands))
    polar = jnp.transpose(pol.reshape(ORB, 2, ORB), (1, 0, 2)).reshape(1, 2, 1, ORB * ORB)
    screened = sum(parts[n].astype(F32) for n in range(NZ)).astype(BF16)
    return polar, screened.reshape(1, 2, 1, ORB, ORB)


def solution(mesh):
    return jax.shard_map(
        on_device,
        mesh=mesh,
        in_specs=(
            P(None, "energy", None, None, "cell"),
            P(None, "energy", None, "cell"),
            P(None, "energy", None, None, "cell"),
            P(),
        ),
        out_specs=(P("cell", None, "energy", None), P("cell", None, "energy", None, None)),
        check_vma=False,
    )
```

```python
import math

import jax
import jax.numpy as jnp
from jax import lax
from jax.experimental import pallas as pl
from jax.experimental.pallas import tpu as pltpu
from jax.sharding import PartitionSpec as P

ORB = 128
NX = 4
NZ = 4
NE = 32
F32 = jnp.float32
BF16 = jnp.bfloat16
MESH = pl.DeviceIdType.MESH
VL = 16 * 1024 * 1024

ROWS = ORB // 4

RD, RC, RN = (0, 1), (2, 1), (4, 1)
LD, LN, LC = (6, 3), (8, 3), (10, 3)
ORDER = (2, 1, 3, 0)


def dot(a, b):
    return lax.dot_general(a, b, (((1,), (0,)), ((), ())), preferred_element_type=F32)


def dot_t(a, b):
    return lax.dot_general(a, b, (((1,), (1,)), ((), ())), preferred_element_type=F32)


def stacked(re, im):
    top = jnp.concatenate([re, im], axis=1)
    bottom = jnp.concatenate([-im, re], axis=1)
    return jnp.concatenate([top, bottom], axis=0)


def kernel(
    g, s, w, cpl, pol, zout,
    gv, sv, cv, srhs, midv, ub, rb, own, zb, zr, ib, il, lb, db, lr, a1, a2, br, bi,
    pb, pr, pg, wx, acc, z2b,
    ld, cld, wld, xs, xr, zs, zrs, es, er, ps, pr_, fr, f1, f2, ws, wr, gs, gr_, z2s, z2r, pols, lcl,
):
    e = lax.axis_index("energy")
    c = lax.axis_index("cell")
    x = lax.div(c, NZ)
    z = lax.rem(c, NZ)

    def xof(dx):
        return lax.rem(x + dx, NX)

    def zof(dz):
        return lax.rem(z + dz, NZ)

    def cell_of(dx, dz):
        return xof(dx) * NZ + zof(dz)

    def rows_of(dx):
        return pl.ds(xof(dx) * NZ, NZ)

    s_load = pltpu.make_async_copy(s, sv, ld.at[4])
    s_load.start()
    c_load = pltpu.make_async_copy(cpl, cv, cld)
    c_load.start()
    g_load = {}
    for n, dx in enumerate((2, 1, 3, 0)):
        g_load[dx] = pltpu.make_async_copy(g.at[:, rows_of(dx)], gv.at[:, rows_of(dx)], ld.at[n])
        g_load[dx].start()
    w_load = pltpu.make_async_copy(w.at[:, rows_of(0)], wx.at[x], wld)
    w_load.start()

    barrier = pltpu.get_barrier_semaphore()

    plane = lax.div(e, 8) * 8
    seat = lax.rem(e, 8)

    def greet(sem):
        for d in (1, NX - 1):
            pl.semaphore_signal(sem, inc=1, device_id={"cell": cell_of(d, 0)}, device_id_type=MESH)
        for d in (2, 6):
            to = plane + lax.rem(seat + d, 8)
            pl.semaphore_signal(sem, inc=1, device_id={"energy": to}, device_id_type=MESH)
        mate = lax.bitwise_xor(e, 1)
        pl.semaphore_signal(sem, inc=1, device_id={"energy": mate}, device_id_type=MESH)
        for d in (1, 15):
            at = lax.rem(lax.div(e, 8) * NZ + z + d, 16)
            to = {"energy": lax.div(at, NZ) * 8 + seat, "cell": x * NZ + lax.rem(at, NZ)}
            pl.semaphore_signal(sem, inc=1, device_id=to, device_id_type=MESH)

    def greet_along_z(sem):
        for d in (8, NE - 8):
            pl.semaphore_signal(
                sem, inc=1, device_id={"energy": lax.rem(e + d, NE)}, device_id_type=MESH
            )

    def heard(sem, count):
        pl.semaphore_wait(sem, count)

    greet(barrier)

    def to_cell(src, dst, ssem, rsem, dx, dz):
        copy = pltpu.make_async_remote_copy(
            src_ref=src, dst_ref=dst, send_sem=ssem, recv_sem=rsem,
            device_id={"cell": cell_of(dx, dz)}, device_id_type=MESH,
        )
        copy.start()
        return copy

    s_load.wait()
    c_load.wait()
    srhs[...] = stacked(sv[0], sv[1])

    def mids(dx):
        g_load[dx].wait()
        rows = rows_of(dx)
        left = jnp.concatenate(
            [gv[0, rows].reshape(NZ * ORB, ORB), gv[1, rows].reshape(NZ * ORB, ORB)], axis=1
        )
        mid = dot(left, srhs[...])
        for zi in range(NZ):
            weight = cv[xof(dx) * NZ + zi, c].astype(F32)
            midv[dx, zi] = (mid[zi * ORB : (zi + 1) * ORB] * weight).astype(BF16)

    def part(dx, zi):
        i = xof(dx) * NZ + zi
        return dot_t(midv[dx, zi], stacked(gv[0, i], gv[1, i]))

    def split(term, out, at, dtype):
        for q in range(4):
            out[q, at, 0] = term[q * ROWS : (q + 1) * ROWS, :ORB].astype(dtype)
            out[q, at, 1] = term[q * ROWS : (q + 1) * ROWS, ORB:].astype(dtype)

    def terms(pair, dest, block):
        for n in range(2):
            split(part(dest, block + n), ub, pair[0] + n, BF16)

    def quarter(t):
        return lax.rem(lax.div(e, 8) + ORDER[t], 4)

    x_sends = []

    def send(pair, t):
        two = pl.ds(pair[0], 2)
        q, n = quarter(t), pair[0] // 2
        x_sends.append(
            to_cell(ub.at[q, two], rb.at[q, two], xs.at[t, n], xr.at[t, n], pair[1], 0)
        )

    def x_arrived(pair, t):
        two = rb.at[quarter(t), pl.ds(pair[0], 2)]
        pltpu.make_async_copy(two, two, xr.at[t, pair[0] // 2]).wait()

    def relay(t):
        q = quarter(t)
        for d, c_pair in ((RD, RC), (LD, LC)):
            x_arrived(d, t)
            two = pl.ds(c_pair[0], 2)
            total = ub[q, two].astype(F32) + rb[q, pl.ds(d[0], 2)].astype(F32)
            ub[q, two] = total.astype(BF16)
            send(c_pair, t)

    def along_z(t):
        q = quarter(t)
        for pair in (RN, LN, RC, LC):
            x_arrived(pair, t)
        total = own[q] + rb[q, pl.ds(2, 4)].astype(F32) + rb[q, pl.ds(8, 4)].astype(F32)
        own[q] = total
        zb[q] = total.astype(BF16)
        for d in (2, 3, 1):
            zi = lax.bitwise_xor(z, d)
            pltpu.make_async_remote_copy(
                src_ref=zb.at[q, zi], dst_ref=zr.at[q, z], send_sem=zs, recv_sem=zrs.at[t, d - 1],
                device_id={"cell": x * NZ + zi}, device_id_type=MESH,
            ).start()

    def send_plane(src, dst, ssem, rsem, dz):
        @pl.loop(1 if dz == 0 else 0, 8)
        def _(n):
            to = lax.rem(plane + 8 * dz, NE) + lax.rem(e + n, 8)
            pltpu.make_async_remote_copy(
                src_ref=src.at[to], dst_ref=dst.at[e], send_sem=ssem, recv_sem=rsem,
                device_id={"energy": to}, device_id_type=MESH,
            ).start()

    def arrived(buf, sem):
        part_of = buf.at[pl.ds(0, NE - 1)]
        pltpu.make_async_copy(part_of, part_of, sem).wait()

    def to_energies(t):
        q = quarter(t)
        total = own[q, z]
        for d in (1, 3, 2):
            n = lax.bitwise_xor(z, d)
            pltpu.make_async_copy(zr.at[q, n], zr.at[q, n], zrs.at[t, d - 1]).wait()
            total = total + zr[q, n].astype(F32)
        il[pl.ds(0, ROWS, 2), :] = total[0]
        il[pl.ds(1, ROWS, 2), :] = total[1]
        tiles = pl.ds(q * 8, 8)
        lb[tiles, 0] = il[...].reshape(8, 8, ORB).astype(BF16)
        lb[tiles, 1] = (il[...] + db[q]).reshape(8, 8, ORB).astype(BF16)
        if ORDER[t] == 0:
            lr[e] = lb[e]
        send_plane(lb, lr, es, er, ORDER[t])

    mids(2)
    terms(RD, 2, 0)
    terms(LD, 2, 2)
    heard(barrier, 7)
    greet(fr.at[0])
    send(RD, 0)
    send(LD, 0)
    mids(1)
    terms(RN, 1, 2)
    send(RN, 0)
    mids(3)
    terms(LN, 3, 0)
    send(LN, 0)
    send(RD, 1)
    send(LD, 1)
    heard(fr.at[0], 7)
    greet(fr.at[1])
    terms(RC, 1, 0)
    terms(LC, 3, 2)
    relay(0)
    send(RN, 1)
    send(LN, 1)
    send(RD, 2)
    send(LD, 2)
    heard(fr.at[1], 7)
    greet(fr.at[2])
    mids(0)
    for zi in range(NZ):
        split(part(0, zi), own, zi, F32)
    relay(1)
    send(RN, 2)
    send(LN, 2)
    send(RD, 3)
    send(LD, 3)
    heard(fr.at[2], 7)
    greet_along_z(f1)
    gr0 = gv[0, c].astype(F32)
    gi0 = gv[1, c].astype(F32)
    ib[pl.ds(0, ORB, 2), :] = gr0 - gr0.T
    ib[pl.ds(1, ORB, 2), :] = gi0 + gi0.T
    db[...] = ib[...].reshape(4, 2 * ROWS, ORB)
    along_z(0)
    relay(2)
    send(RN, 3)
    send(LN, 3)
    along_z(1)
    heard(f1, 2)
    greet_along_z(f2)
    relay(3)

    w_sends = []
    for n, dx in enumerate((1, 3, 2)):
        w_sends.append(to_cell(w.at[:, rows_of(dx)], wx.at[x], ws.at[n], wr.at[n], dx, 0))

    along_z(2)
    heard(f2, 2)
    to_energies(0)
    along_z(3)
    to_energies(1)
    to_energies(2)
    to_energies(3)

    even = lax.rem(lax.broadcasted_iota(jnp.int32, (NE, 8, ORB), 1), 2) == 0

    def row_after(v):
        return pltpu.roll(v, 7, 1)

    def row_before(v):
        return pltpu.roll(v, 1, 1)

    a1[pl.ds(NE, 8)] = jnp.zeros((8, 8, ORB), F32)
    a2[pl.ds(NE, 8)] = jnp.zeros((8, 8, ORB), F32)
    arrived(lr, er)
    low = lr[:, 0].astype(F32)
    high = lr[:, 1].astype(F32) * (1.0 / math.sqrt(NE))
    a1[pl.ds(0, NE)] = jnp.where(even, row_after(low), -row_before(low))
    a2[pl.ds(0, NE)] = -low
    br[...] = jnp.where(even, high, row_before(high))
    bi[...] = jnp.where(even, row_after(high), high)

    for dz in (2, 1, 3, 0):
        first = lax.rem(plane + 8 * dz, NE)

        def eight(block, total, first=first):
            for n in range(8):
                at = block * 8 + n
                window = pl.ds(first + at, 8)
                total = total + a1[window] * br[at] + a2[window] * bi[at]
            return total

        total = lax.fori_loop(0, lax.div(NE - first, 8), eight, jnp.zeros((8, 8, ORB), F32))
        pb[pl.ds(first, 8)] = total.astype(BF16)
        if dz == 0:
            pr[e] = pb[e]
        send_plane(pb, pr, ps, pr_.at[dz], dz)

    for n in range(3):
        pltpu.make_async_copy(wx.at[0], wx.at[0], wr.at[n]).wait()
    w_load.wait()

    g_sends = []
    for dz in (0, 1, 3, 2):
        tiles = pl.ds(lax.rem(plane + (NE - 8 * dz), NE), 8)
        came = pr.at[pl.ds(0, 7 if dz == 0 else 8)]
        pltpu.make_async_copy(came, came, pr_.at[dz]).wait()
        for n, dx in enumerate((2, 1, 3)):
            g_sends.append(to_cell(pr.at[tiles], pg.at[x, tiles], gs.at[n], gr_.at[n], dx, 0))
    pol_out = pltpu.make_async_copy(pr, pol, pols)
    pol_out.start()

    z_sends = []
    recv_of = {2: 0, 3: 1, 1: 2}
    for dx in (0, 1, 3, 2):
        j = xof(dx)
        if dx == 0:
            raw = pr[...]
        else:
            n = recv_of[dx]
            pltpu.make_async_copy(pg.at[j], pg.at[j], gr_.at[n]).wait()
            raw = pg[j]
        ib[...] = raw.astype(F32).reshape(2 * ORB, ORB)
        rhs = stacked(ib[pl.ds(0, ORB, 2), :].astype(BF16), ib[pl.ds(1, ORB, 2), :].astype(BF16))
        left = jnp.concatenate(
            [wx[j, 0].reshape(NZ * ORB, ORB), wx[j, 1].reshape(NZ * ORB, ORB)], axis=1
        )
        mid = dot(left, rhs)
        for zi in range(NZ):
            weight = cv[x * NZ + zi, j * NZ + z].astype(F32)
            midv[dx, zi] = (mid[zi * ORB : (zi + 1) * ORB] * weight).astype(BF16)
        for n, dz in enumerate((2, 3, 1, 0)):
            zi = lax.bitwise_xor(z, dz)
            term = dot_t(midv[dx, zi], stacked(wx[j, 0, zi], wx[j, 1, zi]))
            if dx == 0:
                acc[dz] = term
            elif dx != 2:
                acc[dz] += term
            else:
                term = term + acc[dz]
                z2b[dz, 0] = term[:, :ORB].astype(BF16)
                z2b[dz, 1] = term[:, ORB:].astype(BF16)
                if dz == 0:
                    local = pltpu.make_async_copy(z2b.at[0], zout.at[z], lcl)
                    local.start()
                else:
                    copy = pltpu.make_async_remote_copy(
                        src_ref=z2b.at[dz], dst_ref=zout.at[z], send_sem=z2s.at[n], recv_sem=z2r.at[n],
                        device_id={"cell": x * NZ + zi}, device_id_type=MESH,
                    )
                    copy.start()
                    z_sends.append(copy)

    for copy in x_sends + w_sends + g_sends + z_sends:
        copy.wait_send()
    for buf, sem in ((lb, es), (pb, ps)):
        arrived(buf, sem)
    three = zb.at[pl.ds(0, 3)]
    pltpu.make_async_copy(three, three, zs).wait()
    for n in range(3):
        pltpu.make_async_copy(zout.at[0], zout.at[0], z2r.at[n]).wait()
    pol_out.wait()
    local.wait()


def finish(parts, pol, screened, pol_out, total, sems):
    pol_copy = pltpu.make_async_copy(pol, pol_out, sems.at[0])
    pol_copy.start()
    total[...] = sum(parts[n].astype(F32) for n in range(NZ)).astype(BF16)
    out_copy = pltpu.make_async_copy(total, screened, sems.at[1])
    out_copy.start()
    pol_copy.wait()
    out_copy.wait()


def on_device(g, s, w, coupling):
    block = (2, ORB, ORB)
    dma = pltpu.SemaphoreType.DMA
    vm = pltpu.VMEM
    operands = (
        g.reshape(2, NX * NZ, ORB, ORB), s.reshape(block), w.reshape(2, NX * NZ, ORB, ORB), coupling
    )
    pol, parts = pl.pallas_call(
        kernel,
        out_shape=(
            jax.ShapeDtypeStruct((NE, 8, ORB), BF16),
            jax.ShapeDtypeStruct((NZ, *block), BF16),
        ),
        in_specs=[pl.BlockSpec(memory_space=pltpu.HBM)] * 4,
        out_specs=(pl.BlockSpec(memory_space=pl.ANY), pl.BlockSpec(memory_space=pl.ANY)),
        scratch_shapes=[
            vm((2, NX * NZ, ORB, ORB), BF16),
            vm(block, BF16),
            pltpu.SMEM((NX * NZ, NX * NZ), jnp.int32),
            vm((2 * ORB, 2 * ORB), BF16),
            vm((NX, NZ, ORB, 2 * ORB), BF16),
            vm((4, 12, 2, ROWS, ORB), BF16),
            vm((4, 12, 2, ROWS, ORB), BF16),
            vm((4, NZ, 2, ROWS, ORB), F32),
            vm((4, NZ, 2, ROWS, ORB), BF16),
            vm((4, NZ, 2, ROWS, ORB), BF16),
            vm((2 * ORB, ORB), F32),
            vm((2 * ROWS, ORB), F32),
            vm((NE, 2, 8, ORB), BF16),
            vm((4, 2 * ROWS, ORB), F32),
            vm((NE, 2, 8, ORB), BF16),
            vm((NE + 8, 8, ORB), F32),
            vm((NE + 8, 8, ORB), F32),
            vm((NE, 8, ORB), F32),
            vm((NE, 8, ORB), F32),
            vm((NE, 8, ORB), BF16),
            vm((NE, 8, ORB), BF16),
            vm((NX, NE, 8, ORB), BF16),
            vm((NX, 2, NZ, ORB, ORB), BF16),
            vm((NZ, ORB, 2 * ORB), F32),
            vm((NZ, *block), BF16),
            dma((5,)),
            dma,
            dma,
            dma((4, 6)),
            dma((4, 6)),
            dma,
            dma((4, 3)),
            dma,
            dma,
            dma,
            dma((4,)),
            pltpu.SemaphoreType.REGULAR((3,)),
            pltpu.SemaphoreType.REGULAR,
            pltpu.SemaphoreType.REGULAR,
            dma((3,)),
            dma((3,)),
            dma((3,)),
            dma((3,)),
            dma((3,)),
            dma((3,)),
            dma,
            dma,
        ],
        compiler_params=pltpu.CompilerParams(collective_id=0, has_side_effects=True, vmem_limit_bytes=VL),
    )(*(pltpu.with_memory_space_constraint(v, pltpu.HBM) for v in operands))
    screened, pol = pl.pallas_call(
        finish,
        out_shape=(jax.ShapeDtypeStruct(block, BF16), jax.ShapeDtypeStruct((NE, 8, ORB), BF16)),
        in_specs=[pl.BlockSpec(memory_space=pltpu.VMEM), pl.BlockSpec(memory_space=pl.ANY)],
        out_specs=(pl.BlockSpec(memory_space=pl.ANY), pl.BlockSpec(memory_space=pl.ANY)),
        scratch_shapes=[vm(block, BF16), dma((2,))],
        compiler_params=pltpu.CompilerParams(vmem_limit_bytes=VL // 4),
    )(parts, pol)
    polar = jnp.transpose(pol.reshape(ORB, 2, ORB), (1, 0, 2)).reshape(1, 2, 1, ORB * ORB)
    return polar, screened.reshape(1, 2, 1, ORB, ORB)


def solution(mesh):
    return jax.shard_map(
        on_device,
        mesh=mesh,
        in_specs=(
            P(None, "energy", None, None, "cell"),
            P(None, "energy", None, "cell"),
            P(None, "energy", None, None, "cell"),
            P(),
        ),
        out_specs=(P("cell", None, "energy", None), P("cell", None, "energy", None, None)),
        check_vma=False,
    )
```

```python
import math

import jax
import jax.numpy as jnp
from jax import lax
from jax.experimental import pallas as pl
from jax.experimental.pallas import tpu as pltpu
from jax.sharding import PartitionSpec as P

ORB = 128
NX = 4
NZ = 4
NE = 32
F32 = jnp.float32
BF16 = jnp.bfloat16
MESH = pl.DeviceIdType.MESH
VL = 16 * 1024 * 1024

ROWS = ORB // 4

RD, RC, RN = (0, 1), (2, 1), (4, 1)
LD, LN, LC = (6, 3), (8, 3), (10, 3)
ORDER = (2, 1, 3, 0)


def dot(a, b):
    return lax.dot_general(a, b, (((1,), (0,)), ((), ())), preferred_element_type=F32)


def dot_t(a, b):
    return lax.dot_general(a, b, (((1,), (1,)), ((), ())), preferred_element_type=F32)


def stacked(re, im):
    top = jnp.concatenate([re, im], axis=1)
    bottom = jnp.concatenate([-im, re], axis=1)
    return jnp.concatenate([top, bottom], axis=0)


def kernel(
    g, s, w, cpl, pol, zout,
    gv, sv, cv, srhs, midv, ub, rb, own, zb, zr, ib, il, lb, db, lr, a1, a2, br, bi,
    pb, pr, pg, prhs, wx, acc, z2b,
    ld, cld, wld, xs, xr, zs, zrs, es, er, ps, pr_, fr, f1, f2, ws, wr, gs, gr_, z2s, z2r, pols, lcl,
):
    e = lax.axis_index("energy")
    c = lax.axis_index("cell")
    x = lax.div(c, NZ)
    z = lax.rem(c, NZ)

    def xof(dx):
        return lax.rem(x + dx, NX)

    def zof(dz):
        return lax.rem(z + dz, NZ)

    def cell_of(dx, dz):
        return xof(dx) * NZ + zof(dz)

    def rows_of(dx):
        return pl.ds(xof(dx) * NZ, NZ)

    s_load = pltpu.make_async_copy(s, sv, ld.at[4])
    s_load.start()
    c_load = pltpu.make_async_copy(cpl, cv, cld)
    c_load.start()
    g_load = {}
    for n, dx in enumerate((2, 1, 3, 0)):
        g_load[dx] = pltpu.make_async_copy(g.at[:, rows_of(dx)], gv.at[:, rows_of(dx)], ld.at[n])
        g_load[dx].start()
    w_load = pltpu.make_async_copy(w.at[:, rows_of(0)], wx.at[x], wld)
    w_load.start()

    barrier = pltpu.get_barrier_semaphore()

    plane = lax.div(e, 8) * 8
    seat = lax.rem(e, 8)

    def greet(sem):
        for d in (1, NX - 1):
            pl.semaphore_signal(sem, inc=1, device_id={"cell": cell_of(d, 0)}, device_id_type=MESH)
        for d in (2, 6):
            to = plane + lax.rem(seat + d, 8)
            pl.semaphore_signal(sem, inc=1, device_id={"energy": to}, device_id_type=MESH)
        mate = lax.bitwise_xor(e, 1)
        pl.semaphore_signal(sem, inc=1, device_id={"energy": mate}, device_id_type=MESH)
        for d in (1, 15):
            at = lax.rem(lax.div(e, 8) * NZ + z + d, 16)
            to = {"energy": lax.div(at, NZ) * 8 + seat, "cell": x * NZ + lax.rem(at, NZ)}
            pl.semaphore_signal(sem, inc=1, device_id=to, device_id_type=MESH)

    def greet_along_z(sem):
        for d in (8, NE - 8):
            pl.semaphore_signal(
                sem, inc=1, device_id={"energy": lax.rem(e + d, NE)}, device_id_type=MESH
            )

    def heard(sem, count):
        pl.semaphore_wait(sem, count)

    greet(barrier)

    def to_cell(src, dst, ssem, rsem, dx, dz):
        copy = pltpu.make_async_remote_copy(
            src_ref=src, dst_ref=dst, send_sem=ssem, recv_sem=rsem,
            device_id={"cell": cell_of(dx, dz)}, device_id_type=MESH,
        )
        copy.start()
        return copy

    s_load.wait()
    c_load.wait()
    srhs[...] = stacked(sv[0], sv[1])

    def mids(dx):
        g_load[dx].wait()
        rows = rows_of(dx)
        left = jnp.concatenate(
            [gv[0, rows].reshape(NZ * ORB, ORB), gv[1, rows].reshape(NZ * ORB, ORB)], axis=1
        )
        mid = dot(left, srhs[...])
        for zi in range(NZ):
            weight = cv[xof(dx) * NZ + zi, c].astype(F32)
            midv[dx, zi] = (mid[zi * ORB : (zi + 1) * ORB] * weight).astype(BF16)

    def part(dx, zi):
        i = xof(dx) * NZ + zi
        return dot_t(midv[dx, zi], stacked(gv[0, i], gv[1, i]))

    def split(term, out, at, dtype):
        for q in range(4):
            out[q, at, 0] = term[q * ROWS : (q + 1) * ROWS, :ORB].astype(dtype)
            out[q, at, 1] = term[q * ROWS : (q + 1) * ROWS, ORB:].astype(dtype)

    def terms(pair, dest, block):
        for n in range(2):
            split(part(dest, block + n), ub, pair[0] + n, BF16)

    def quarter(t):
        return lax.rem(lax.div(e, 8) + ORDER[t], 4)

    x_sends = []

    def send(pair, t):
        two = pl.ds(pair[0], 2)
        q, n = quarter(t), pair[0] // 2
        x_sends.append(
            to_cell(ub.at[q, two], rb.at[q, two], xs.at[t, n], xr.at[t, n], pair[1], 0)
        )

    def x_arrived(pair, t):
        two = rb.at[quarter(t), pl.ds(pair[0], 2)]
        pltpu.make_async_copy(two, two, xr.at[t, pair[0] // 2]).wait()

    def relay(t):
        q = quarter(t)
        for d, c_pair in ((RD, RC), (LD, LC)):
            x_arrived(d, t)
            two = pl.ds(c_pair[0], 2)
            total = ub[q, two].astype(F32) + rb[q, pl.ds(d[0], 2)].astype(F32)
            ub[q, two] = total.astype(BF16)
            send(c_pair, t)

    def along_z(t):
        q = quarter(t)
        for pair in (RN, LN, RC, LC):
            x_arrived(pair, t)
        total = own[q] + rb[q, pl.ds(2, 4)].astype(F32) + rb[q, pl.ds(8, 4)].astype(F32)
        own[q] = total
        zb[q] = total.astype(BF16)
        for d in (2, 3, 1):
            zi = lax.bitwise_xor(z, d)
            pltpu.make_async_remote_copy(
                src_ref=zb.at[q, zi], dst_ref=zr.at[q, z], send_sem=zs, recv_sem=zrs.at[t, d - 1],
                device_id={"cell": x * NZ + zi}, device_id_type=MESH,
            ).start()

    def send_plane(src, dst, ssem, rsem, dz):
        @pl.loop(1 if dz == 0 else 0, 8)
        def _(n):
            to = lax.rem(plane + 8 * dz, NE) + lax.rem(e + n, 8)
            pltpu.make_async_remote_copy(
                src_ref=src.at[to], dst_ref=dst.at[e], send_sem=ssem, recv_sem=rsem,
                device_id={"energy": to}, device_id_type=MESH,
            ).start()

    def arrived(buf, sem):
        part_of = buf.at[pl.ds(0, NE - 1)]
        pltpu.make_async_copy(part_of, part_of, sem).wait()

    def to_energies(t):
        q = quarter(t)
        total = own[q, z]
        for d in (1, 3, 2):
            n = lax.bitwise_xor(z, d)
            pltpu.make_async_copy(zr.at[q, n], zr.at[q, n], zrs.at[t, d - 1]).wait()
            total = total + zr[q, n].astype(F32)
        il[pl.ds(0, ROWS, 2), :] = total[0]
        il[pl.ds(1, ROWS, 2), :] = total[1]
        tiles = pl.ds(q * 8, 8)
        lb[tiles, 0] = il[...].reshape(8, 8, ORB).astype(BF16)
        lb[tiles, 1] = (il[...] + db[q]).reshape(8, 8, ORB).astype(BF16)
        if ORDER[t] == 0:
            lr[e] = lb[e]
        send_plane(lb, lr, es, er, ORDER[t])

    mids(2)
    terms(RD, 2, 0)
    terms(LD, 2, 2)
    heard(barrier, 7)
    greet(fr.at[0])
    send(RD, 0)
    send(LD, 0)
    mids(1)
    terms(RN, 1, 2)
    send(RN, 0)
    mids(3)
    terms(LN, 3, 0)
    send(LN, 0)
    send(RD, 1)
    send(LD, 1)
    heard(fr.at[0], 7)
    greet(fr.at[1])
    terms(RC, 1, 0)
    terms(LC, 3, 2)
    relay(0)
    send(RN, 1)
    send(LN, 1)
    send(RD, 2)
    send(LD, 2)
    heard(fr.at[1], 7)
    greet(fr.at[2])
    mids(0)
    for zi in range(NZ):
        split(part(0, zi), own, zi, F32)
    relay(1)
    send(RN, 2)
    send(LN, 2)
    send(RD, 3)
    send(LD, 3)
    heard(fr.at[2], 7)
    greet_along_z(f1)
    gr0 = gv[0, c].astype(F32)
    gi0 = gv[1, c].astype(F32)
    ib[pl.ds(0, ORB, 2), :] = gr0 - gr0.T
    ib[pl.ds(1, ORB, 2), :] = gi0 + gi0.T
    db[...] = ib[...].reshape(4, 2 * ROWS, ORB)
    along_z(0)
    relay(2)
    send(RN, 3)
    send(LN, 3)
    along_z(1)
    heard(f1, 2)
    greet_along_z(f2)
    relay(3)

    w_sends = []
    for n, dx in enumerate((1, 3, 2)):
        w_sends.append(to_cell(w.at[:, rows_of(dx)], wx.at[x], ws.at[n], wr.at[n], dx, 0))

    along_z(2)
    along_z(3)
    heard(f2, 2)
    to_energies(0)
    to_energies(1)
    to_energies(2)
    to_energies(3)

    even = lax.rem(lax.broadcasted_iota(jnp.int32, (NE, 8, ORB), 1), 2) == 0

    def row_after(v):
        return pltpu.roll(v, 7, 1)

    def row_before(v):
        return pltpu.roll(v, 1, 1)

    a1[pl.ds(NE, 8)] = jnp.zeros((8, 8, ORB), F32)
    a2[pl.ds(NE, 8)] = jnp.zeros((8, 8, ORB), F32)
    arrived(lr, er)
    low = lr[:, 0].astype(F32)
    high = lr[:, 1].astype(F32) * (1.0 / math.sqrt(NE))
    a1[pl.ds(0, NE)] = jnp.where(even, row_after(low), -row_before(low))
    a2[pl.ds(0, NE)] = -low
    br[...] = jnp.where(even, high, row_before(high))
    bi[...] = jnp.where(even, row_after(high), high)

    for dz in (2, 1, 3, 0):
        first = lax.rem(plane + 8 * dz, NE)

        def eight(block, total, first=first):
            for n in range(8):
                at = block * 8 + n
                window = pl.ds(first + at, 8)
                total = total + a1[window] * br[at] + a2[window] * bi[at]
            return total

        total = lax.fori_loop(0, lax.div(NE - first, 8), eight, jnp.zeros((8, 8, ORB), F32))
        pb[pl.ds(first, 8)] = total.astype(BF16)
        if dz == 0:
            pr[e] = pb[e]
        send_plane(pb, pr, ps, pr_.at[dz], dz)

    for n in range(3):
        pltpu.make_async_copy(wx.at[0], wx.at[0], wr.at[n]).wait()
    w_load.wait()

    g_sends = []
    for dz in (0, 1, 3, 2):
        tiles = pl.ds(lax.rem(plane + (NE - 8 * dz), NE), 8)
        came = pr.at[pl.ds(0, 7 if dz == 0 else 8)]
        pltpu.make_async_copy(came, came, pr_.at[dz]).wait()
        for n, dx in enumerate((2, 1, 3)):
            g_sends.append(to_cell(pr.at[tiles], pg.at[x, tiles], gs.at[n], gr_.at[n], dx, 0))
    pol_out = pltpu.make_async_copy(pr, pol, pols)
    pol_out.start()

    z_sends = []
    recv_of = {2: 0, 3: 1, 1: 2}
    for pair in ((2, 3), (1, 0)):
        for dx in (0, 1, 3, 2):
            j = xof(dx)
            if pair[0] == 2:
                if dx == 0:
                    raw = pr[...]
                else:
                    pltpu.make_async_copy(pg.at[j], pg.at[j], gr_.at[recv_of[dx]]).wait()
                    raw = pg[j]
                ib[...] = raw.astype(F32).reshape(2 * ORB, ORB)
                prhs[dx] = stacked(
                    ib[pl.ds(0, ORB, 2), :].astype(BF16), ib[pl.ds(1, ORB, 2), :].astype(BF16)
                )
            blocks = [lax.bitwise_xor(z, d) for d in pair]
            left = jnp.concatenate(
                [jnp.concatenate([wx[j, 0, zi], wx[j, 1, zi]], axis=1) for zi in blocks], axis=0
            )
            mid = dot(left, prhs[dx])
            for n, (d, zi) in enumerate(zip(pair, blocks)):
                weight = cv[x * NZ + zi, j * NZ + z].astype(F32)
                half = (mid[n * ORB : (n + 1) * ORB] * weight).astype(BF16)
                term = dot_t(half, stacked(wx[j, 0, zi], wx[j, 1, zi]))
                if dx == 0:
                    acc[d] = term
                elif dx != 2:
                    acc[d] += term
                else:
                    term = term + acc[d]
                    z2b[d, 0] = term[:, :ORB].astype(BF16)
                    z2b[d, 1] = term[:, ORB:].astype(BF16)
                    if d == 0:
                        local = pltpu.make_async_copy(z2b.at[0], zout.at[z], lcl)
                        local.start()
                    else:
                        copy = pltpu.make_async_remote_copy(
                            src_ref=z2b.at[d], dst_ref=zout.at[z], send_sem=z2s.at[d - 1],
                            recv_sem=z2r.at[d - 1], device_id={"cell": x * NZ + zi}, device_id_type=MESH,
                        )
                        copy.start()
                        z_sends.append(copy)

    for copy in x_sends + w_sends + g_sends + z_sends:
        copy.wait_send()
    for buf, sem in ((lb, es), (pb, ps)):
        arrived(buf, sem)
    three = zb.at[pl.ds(0, 3)]
    pltpu.make_async_copy(three, three, zs).wait()
    for n in range(3):
        pltpu.make_async_copy(zout.at[0], zout.at[0], z2r.at[n]).wait()
    pol_out.wait()
    local.wait()


def finish(parts, pol, screened, pol_out, total, sems):
    pol_copy = pltpu.make_async_copy(pol, pol_out, sems.at[0])
    pol_copy.start()
    total[...] = sum(parts[n].astype(F32) for n in range(NZ)).astype(BF16)
    out_copy = pltpu.make_async_copy(total, screened, sems.at[1])
    out_copy.start()
    pol_copy.wait()
    out_copy.wait()


def on_device(g, s, w, coupling):
    block = (2, ORB, ORB)
    dma = pltpu.SemaphoreType.DMA
    vm = pltpu.VMEM
    operands = (
        g.reshape(2, NX * NZ, ORB, ORB), s.reshape(block), w.reshape(2, NX * NZ, ORB, ORB), coupling
    )
    pol, parts = pl.pallas_call(
        kernel,
        out_shape=(
            jax.ShapeDtypeStruct((NE, 8, ORB), BF16),
            jax.ShapeDtypeStruct((NZ, *block), BF16),
        ),
        in_specs=[pl.BlockSpec(memory_space=pltpu.HBM)] * 4,
        out_specs=(pl.BlockSpec(memory_space=pl.ANY), pl.BlockSpec(memory_space=pl.ANY)),
        scratch_shapes=[
            vm((2, NX * NZ, ORB, ORB), BF16),
            vm(block, BF16),
            pltpu.SMEM((NX * NZ, NX * NZ), jnp.int32),
            vm((2 * ORB, 2 * ORB), BF16),
            vm((NX, NZ, ORB, 2 * ORB), BF16),
            vm((4, 12, 2, ROWS, ORB), BF16),
            vm((4, 12, 2, ROWS, ORB), BF16),
            vm((4, NZ, 2, ROWS, ORB), F32),
            vm((4, NZ, 2, ROWS, ORB), BF16),
            vm((4, NZ, 2, ROWS, ORB), BF16),
            vm((2 * ORB, ORB), F32),
            vm((2 * ROWS, ORB), F32),
            vm((NE, 2, 8, ORB), BF16),
            vm((4, 2 * ROWS, ORB), F32),
            vm((NE, 2, 8, ORB), BF16),
            vm((NE + 8, 8, ORB), F32),
            vm((NE + 8, 8, ORB), F32),
            vm((NE, 8, ORB), F32),
            vm((NE, 8, ORB), F32),
            vm((NE, 8, ORB), BF16),
            vm((NE, 8, ORB), BF16),
            vm((NX, NE, 8, ORB), BF16),
            vm((NX, 2 * ORB, 2 * ORB), BF16),
            vm((NX, 2, NZ, ORB, ORB), BF16),
            vm((NZ, ORB, 2 * ORB), F32),
            vm((NZ, *block), BF16),
            dma((5,)),
            dma,
            dma,
            dma((4, 6)),
            dma((4, 6)),
            dma,
            dma((4, 3)),
            dma,
            dma,
            dma,
            dma((4,)),
            pltpu.SemaphoreType.REGULAR((3,)),
            pltpu.SemaphoreType.REGULAR,
            pltpu.SemaphoreType.REGULAR,
            dma((3,)),
            dma((3,)),
            dma((3,)),
            dma((3,)),
            dma((3,)),
            dma((3,)),
            dma,
            dma,
        ],
        compiler_params=pltpu.CompilerParams(collective_id=0, has_side_effects=True, vmem_limit_bytes=VL),
    )(*(pltpu.with_memory_space_constraint(v, pltpu.HBM) for v in operands))
    screened, pol = pl.pallas_call(
        finish,
        out_shape=(jax.ShapeDtypeStruct(block, BF16), jax.ShapeDtypeStruct((NE, 8, ORB), BF16)),
        in_specs=[pl.BlockSpec(memory_space=pltpu.VMEM), pl.BlockSpec(memory_space=pl.ANY)],
        out_specs=(pl.BlockSpec(memory_space=pl.ANY), pl.BlockSpec(memory_space=pl.ANY)),
        scratch_shapes=[vm(block, BF16), dma((2,))],
        compiler_params=pltpu.CompilerParams(vmem_limit_bytes=VL // 4),
    )(parts, pol)
    polar = jnp.transpose(pol.reshape(ORB, 2, ORB), (1, 0, 2)).reshape(1, 2, 1, ORB * ORB)
    return polar, screened.reshape(1, 2, 1, ORB, ORB)


def solution(mesh):
    return jax.shard_map(
        on_device,
        mesh=mesh,
        in_specs=(
            P(None, "energy", None, None, "cell"),
            P(None, "energy", None, "cell"),
            P(None, "energy", None, None, "cell"),
            P(),
        ),
        out_specs=(P("cell", None, "energy", None), P("cell", None, "energy", None, None)),
        check_vma=False,
    )
```
